256 devices in a mesh: energy: 32 (over z, y), slab: 8 (over x, core).
Axes of the slice: x: 4, y: 4, z: 8, core: 2. Of those that a mesh axis runs over, the one named last changes fastest.
Arguments:
- green_prev: bfloat16 [32, 8, 2, 512, 512], P('energy', 'slab'), may hold values from -6 to 6
- slab_inverse: bfloat16 [8, 2, 512, 512], P('slab')
- coupling_block: bfloat16 [512, 512], replicated
- phonon_coupling: bfloat16 [4, 512, 512], P(None, 'energy'), may hold values from -0.1796875 to 0.1796875
- offset: float32 [32], P('energy'), may hold values from -0.5 to 0.5
- occupation: float32 [32], P('energy'), may hold values from 0.05 to 1
- pair_source: int32 [32, 6], replicated, may hold values from 0 to 31
- pair_mode: int32 [32, 6], replicated, may hold values from 0 to 3
- active_slabs: int32 [32], P('energy'), may hold values from 1 to 8, as said below
Outputs:
- green_new: bfloat16 [32, 8, 2, 512, 512], P('energy', 'slab')
- density: float32 [8, 512], P('slab')
The draws below stay inside these ranges and needn't reach their ends.
Inputs may be any that keep to these rules, and one draw needn't show every extreme that they name: `active_slabs`: some energy scatters in all 8 slabs.
All inputs are finite; a program needn't handle non-finite values.
Results may differ from the reference program's by a relative error of at most 0.012.
Values may be sent and summed in bfloat16 or wider, within the bound.
A program may use at most 128 MiB of HBM per device.

```python
import math
import jax
import jax.numpy as jnp
import numpy as np
from jax import lax

ORBITALS = 512
MODES = 4
PAIRS = 6
ENERGIES = 32
SLABS = 8


def draw_slab_inverse(key, part):
    key_list = jax.random.split(key, 3)
    shape_full = (SLABS, ORBITALS, ORBITALS)
    noise_real = jax.random.normal(key_list[0], shape_full, jnp.float32)
    noise_imag = jax.random.normal(key_list[1], shape_full, jnp.float32)
    spread = 0.3 / math.sqrt(ORBITALS)
    diagonal_gain = jax.random.uniform(key_list[2], (SLABS, ORBITALS), jnp.float32, 0.7, 1.3)
    identity_matrix = jnp.eye(ORBITALS, dtype=jnp.float32)
    real_block = noise_real * spread + diagonal_gain[:, :, None] * identity_matrix[None]
    imag_block = noise_imag * spread
    return jnp.stack((real_block, imag_block), axis=1).astype(jnp.bfloat16)


def draw_coupling_block(key, part):
    key_list = jax.random.split(key, 2)
    noise_block = jax.random.normal(key_list[0], (ORBITALS, ORBITALS), jnp.float32)
    diagonal_gain = jax.random.uniform(key_list[1], (ORBITALS,), jnp.float32, 0.8, 1.2)
    identity_matrix = jnp.eye(ORBITALS, dtype=jnp.float32)
    block_value = 0.55 * diagonal_gain[:, None] * identity_matrix + noise_block * (0.2 / math.sqrt(ORBITALS))
    return block_value.astype(jnp.bfloat16)


def draw_active_slabs(key, part):
    key_list = jax.random.split(key, 2)
    values_drawn = jax.random.randint(key_list[0], (ENERGIES,), 1, SLABS + 1, dtype=jnp.int32)
    chosen = jax.random.randint(key_list[1], (), 0, ENERGIES, dtype=jnp.int32)
    positions = jnp.arange(ENERGIES, dtype=jnp.int32)
    return jnp.where(positions == chosen, jnp.int32(SLABS), values_drawn).astype(jnp.int32)


def touch_ends(entries, key, least, largest):
    spot = [jax.random.randint(jax.random.fold_in(key, axis), (), 0, length) for axis, length in enumerate(entries.shape)]
    widest = entries.shape.index(max(entries.shape))
    next_to = spot[:widest] + [(spot[widest] + 1) % entries.shape[widest]] + spot[widest + 1:]
    return entries.at[tuple(spot)].set(least).at[tuple(next_to)].set(largest)


def block_scale(own_key, extent, cuts, least, high):
    gain = 1.0
    for axis_at, parts in cuts:
        draws = jax.random.uniform(jax.random.fold_in(jax.random.fold_in(own_key, 6), axis_at), (parts,), jnp.float32, least / len(cuts), high / len(cuts))
        gain = gain * jnp.repeat(jnp.exp(draws), extent[axis_at] // parts).reshape((-1,) + (1,) * (len(extent) - 1 - axis_at))
    return gain


def cumulative_ranks(number_of, lean):
    weights = [(1 << 20) // math.isqrt(rank ** lean) + 1 for rank in range(1, number_of + 1)]
    scale = 1 + sum(weights) // (1 << 30)
    return np.cumsum(np.array([max(1, weight // scale) for weight in weights]))


def ranked(key, shape, amount, lean):
    listing = cumulative_ranks(amount, lean)
    lot = jax.random.randint(jax.random.fold_in(key, 1), shape, 0, int(listing[amount - 1]))
    standing = jnp.searchsorted(jnp.asarray(listing, jnp.int32), lot, side="right")
    return jax.random.permutation(jax.random.fold_in(key, 2), amount)[standing].astype(jnp.int32)


def scatter_about(key, shape, width, bound, pieces=(), kind=jnp.bfloat16):
    entries = jax.random.normal(key, shape, jnp.float32) * width
    if len(pieces) > 0:
        entries = block_scale(key, shape, pieces, -0.22, 0.18) * entries
    return jnp.clip(entries, min=-bound, max=bound).astype(kind)


def setup_inputs(seed: int = 0) -> dict:
    key_of = jax.random.split(jax.random.key(seed), 10)
    return {
        "green_prev": scatter_about(key_of[0], (ENERGIES, SLABS, 2, ORBITALS, ORBITALS), 1.0, 6.0, ((0, 32), (1, 8))),
        "slab_inverse": draw_slab_inverse(jax.random.fold_in(key_of[9], 71), 0),
        "coupling_block": draw_coupling_block(jax.random.fold_in(key_of[9], 71), 0),
        "phonon_coupling": scatter_about(key_of[3], (MODES, ORBITALS, ORBITALS), 0.03, 0.1796875, ((1, 32),)),
        "offset": jnp.clip(jax.random.uniform(key_of[4], (ENERGIES,), jnp.float32, -0.5, 0.5) * block_scale(key_of[4], (ENERGIES,), ((0, 32),), -0.4, 0.0), -0.5, 0.5),
        "occupation": jnp.clip(jnp.exp(math.log(1.0) - 2.9957323 * jax.random.uniform(key_of[5], (ENERGIES,), jnp.float32) ** block_scale(key_of[5], (ENERGIES,), ((0, 32),), -0.2, 0.2)), 0.05, 1.0),
        "pair_source": touch_ends(ranked(key_of[6], (ENERGIES, PAIRS), ENERGIES, 1), jax.random.fold_in(key_of[6], 3), 0, ENERGIES - 1).astype(jnp.int32),
        "pair_mode": touch_ends(jax.random.randint(key_of[7], (ENERGIES, PAIRS), 0, MODES), jax.random.fold_in(key_of[7], 1), 0, MODES - 1).astype(jnp.int32),
        "active_slabs": draw_active_slabs(jax.random.fold_in(key_of[9], 71), 0),
    }


def complex_dot(first_real, first_imag, second_real, second_imag):
    real_part = jnp.dot(first_real, second_real, preferred_element_type=jnp.float32) - jnp.dot(first_imag, second_imag, preferred_element_type=jnp.float32)
    imag_part = jnp.dot(first_real, second_imag, preferred_element_type=jnp.float32) + jnp.dot(first_imag, second_real, preferred_element_type=jnp.float32)
    return jnp.stack((real_part, imag_part))


def reference(green_prev, slab_inverse, coupling_block, phonon_coupling, offset, occupation, pair_source, pair_mode, active_slabs):
    energy_iota = jnp.arange(ENERGIES, dtype=jnp.int32)
    mode_iota = jnp.arange(MODES, dtype=jnp.int32)
    source_hot = (pair_source[:, :, None] == energy_iota[None, None, :]).astype(jnp.float32)
    mode_hot = (pair_mode[:, :, None] == mode_iota[None, None, :]).astype(jnp.float32)
    weights = jnp.einsum('epf,epm->mef', source_hot, mode_hot).astype(jnp.bfloat16)

    def mix_slab(green_slab):
        flat_rows = green_slab.reshape(ENERGIES, -1)
        summed = jnp.zeros(green_slab.shape, jnp.float32)
        for mode_index in range(MODES):
            combined = jnp.dot(weights[mode_index], flat_rows, preferred_element_type=jnp.float32).reshape(green_slab.shape)
            summed = summed + phonon_coupling[mode_index].astype(jnp.float32)[None, None] * combined
        return summed.astype(jnp.bfloat16)

    self_energy = jnp.moveaxis(lax.map(mix_slab, jnp.moveaxis(green_prev, 1, 0)), 0, 1)

    def couple_slab(block):
        return jnp.stack((jnp.dot(block[0], coupling_block, preferred_element_type=jnp.float32), jnp.dot(block[1], coupling_block, preferred_element_type=jnp.float32))).astype(jnp.bfloat16)

    couple = lax.map(couple_slab, slab_inverse)
    identity_matrix = jnp.eye(ORBITALS, dtype=jnp.float32)
    slab_iota = jnp.arange(SLABS, dtype=jnp.int32)

    def per_energy(items):
        energy_sigma, energy_offset, energy_active = items

        def advance(carry, slab_items):
            inverse, factor, sigma_block, position = slab_items
            active_mask = (position < energy_active).astype(jnp.float32)
            total_real = active_mask * sigma_block[0].astype(jnp.float32) + energy_offset * identity_matrix
            total_imag = active_mask * sigma_block[1].astype(jnp.float32)
            sig_total = jnp.stack((total_real, total_imag)).astype(jnp.bfloat16)
            half_product = complex_dot(inverse[0], inverse[1], sig_total[0], sig_total[1]).astype(jnp.bfloat16)
            base_block = inverse.astype(jnp.float32) + complex_dot(half_product[0], half_product[1], inverse[0], inverse[1])
            left_block = complex_dot(factor[0], factor[1], carry[0], carry[1]).astype(jnp.bfloat16)
            right_block = complex_dot(left_block[0], left_block[1], factor[0].T, factor[1].T)
            fresh = (right_block + base_block).astype(jnp.bfloat16)
            return fresh, fresh

        start = jnp.zeros((2, ORBITALS, ORBITALS), jnp.bfloat16)
        final_block, blocks = lax.scan(advance, start, (slab_inverse, couple, energy_sigma, slab_iota))
        return blocks

    green_new = lax.map(per_energy, (self_energy, offset, active_slabs))
    diagonal_imag = jnp.diagonal(green_new[:, :, 1].astype(jnp.float32), axis1=-2, axis2=-1)
    density = -jnp.einsum('e,esn->sn', occupation.astype(jnp.float32), diagonal_imag)
    return green_new, density
```

```python
import functools

import jax
import jax.numpy as jnp
from jax import lax
from jax.experimental import pallas as pl
from jax.experimental.pallas import tpu as pltpu
from jax.sharding import PartitionSpec as P

MESH = pl.DeviceIdType.MESH
CHUNKS = 4
BF16 = jnp.bfloat16
F32 = jnp.float32


def dot(a, b):
    return jnp.dot(a, b, preferred_element_type=F32)


def dot_nt(a, b):
    return lax.dot_general(a, b, (((1,), (1,)), ((), ())), preferred_element_type=F32)


def kernel(
    sizes,
    green, inv, coup, phon, off, occ, src, mode, act,
    out, dens, *scratch,
):
    E, NS, N, K, NM, NP, NY = sizes
    recvs = scratch[:K]
    (
        sigout, S, psend, left, QR, QI, prev, V, phonf, C, Cp, tmp, mrecv, msend, acc, ostage, dsend, drecv,
        load_sem, own_sem, a1s, a1r, a2s, a2r, prs, prr, ms, mr, mfs, sps, spr, pss, psf, prl, prc, out_sem, ds, dr,
    ) = scratch[K:]
    NZ = E // NY
    R = N // E
    W = N // K
    NX = NS // 2
    e = lax.axis_index("energy")
    s = lax.axis_index("slab")
    z, y = e // NY, e % NY
    x, core = s // 2, s % 2
    T = min(256, N)

    def peer_of(k):
        i = k % NZ
        j = k // NZ
        dz = (i % 2) * ((i + 1) // 2) + (1 - i % 2) * ((NZ - i // 2) % NZ)
        return ((z + dz) % NZ) * NY + (y + j) % NY

    barrier = pltpu.get_barrier_semaphore()

    def greet(k, _):
        pl.semaphore_signal(barrier, inc=1, device_id=(peer_of(k), s), device_id_type=MESH)
        return 0

    lax.fori_loop(1, E, greet, 0)

    def greet_x(k, _):
        pl.semaphore_signal(barrier, inc=1, device_id=(e, (s + k) % NS), device_id_type=MESH)
        return 0

    lax.fori_loop(1, NS, greet_x, 0)

    load_inv = pltpu.make_async_copy(inv.at[0], left.at[0], load_sem.at[0])
    load_inv.start()
    load_v = pltpu.make_async_copy(coup, V, load_sem.at[1])
    load_v.start()
    my_rows = pl.ds(pl.multiple_of(e * R, R), R)
    own = []
    for c in range(K):
        own.append(
            pltpu.make_async_copy(green.at[0, 0, :, my_rows, pl.ds(c * W, W)], recvs[c].at[e], own_sem.at[c])
        )
        own[-1].start()
    for c in range(K):
        phonf[c] = phon[:, :, c * W:(c + 1) * W].astype(F32)

    pl.semaphore_wait(barrier, E - 1 + NS - 1)

    def send_rows(c):
        def one(k, _):
            p = peer_of(k)
            pltpu.make_async_remote_copy(
                src_ref=green.at[0, 0, :, pl.ds(pl.multiple_of(p * R, R), R), pl.ds(pl.multiple_of(c * W, W), W)],
                dst_ref=recvs[c].at[e],
                send_sem=a1s.at[c],
                recv_sem=a1r.at[c],
                device_id=(p, s),
                device_id_type=MESH,
            ).start()
            return 0

        lax.fori_loop(1, E, one, 0)

    def send_sigma(c):
        def one(k, _):
            p = peer_of(k)
            pltpu.make_async_remote_copy(
                src_ref=sigout.at[c, p],
                dst_ref=S.at[0, c, my_rows, :],
                send_sem=a2s.at[c],
                recv_sem=a2r.at[c],
                device_id=(p, s),
                device_id_type=MESH,
            ).start()
            return 0

        lax.fori_loop(1, E, one, 0)

    def wait_bytes(ref, sem):
        pltpu.make_async_copy(ref, ref, sem).wait()

    send_rows(0)
    send_rows(1)
    to_partner = pltpu.make_async_remote_copy(
        src_ref=inv.at[0], dst_ref=prev, send_sem=prs, recv_sem=prr, device_id=(e, s + 1 - 2 * core), device_id_type=MESH
    )

    @pl.when(core == 0)
    def _():
        to_partner.start()

    def cmul(dst, a, b, nt=False):
        def tile(j, _):
            at = pl.ds(pl.multiple_of(j * T, T), T)
            if nt:
                br, bi, mm = b[0, at, :], b[1, at, :], dot_nt
            else:
                br, bi, mm = b[0, :, at], b[1, :, at], dot
            ar, ai = a[0], a[1]
            dst[0, :, at] = (mm(ar, br) - mm(ai, bi)).astype(dst.dtype)
            dst[1, :, at] = (mm(ar, bi) + mm(ai, br)).astype(dst.dtype)
            return 0

        lax.fori_loop(0, N // T, tile, 0)

    def stack_rows(slot, q):
        def one(c, _):
            at = pl.ds(pl.multiple_of(c * W, W), W)
            QR[slot, c, :W, :] = q[0, at, :]
            QR[slot, c, W:, :] = q[1, at, :]
            QI[slot, c, :W, :] = q[1, at, :]
            QI[slot, c, W:, :] = q[0, at, :]
            return 0

        lax.fori_loop(0, K, one, 0)

    def stack_transposed(slot, q):
        def one(c, _):
            at = pl.ds(pl.multiple_of(c * W, W), W)
            tr = q[0, :, at].astype(F32).T.astype(BF16)
            ti = q[1, :, at].astype(F32).T.astype(BF16)
            QR[slot, c, :W, :] = tr
            QR[slot, c, W:, :] = ti
            QI[slot, c, :W, :] = ti
            QI[slot, c, W:, :] = tr
            return 0

        lax.fori_loop(0, K, one, 0)

    def couple(dst, a):
        def one(k, _):
            dst[k] = dot(a[k], V[...]).astype(BF16)
            return 0

        lax.fori_loop(0, 2, one, 0)

    def absorb(slot, c, chunk):
        u = dot(left[slot, 0], chunk)
        v = dot(left[slot, 1], chunk)
        hr = (u[:, :W] - v[:, W:]).astype(BF16)
        hi = (u[:, W:] + v[:, :W]).astype(BF16)
        acc[0] += dot(jnp.concatenate((hr, -hi), axis=1), QR[slot, c])
        acc[1] += dot(jnp.concatenate((hr, hi), axis=1), QI[slot, c])

    load_inv.wait()
    load_v.wait()
    couple(C, left.at[0])
    stack_rows(0, left.at[0])
    acc[...] = left[0].astype(F32)

    def send_m(to_x):
        return pltpu.make_async_remote_copy(
            src_ref=msend, dst_ref=mrecv.at[x - 1], send_sem=ms.at[to_x], recv_sem=mr.at[x - 1],
            device_id=(e, 2 * to_x + 1), device_id_type=MESH,
        )

    def pair_setup():
        @pl.when(core == 1)
        def _():
            to_partner.wait_recv()
            couple(Cp, prev)
            cmul(left.at[1], C, prev)
            cmul(tmp, prev, C, nt=True)
            stack_rows(1, tmp)

            def tile(j, _):
                at = pl.ds(pl.multiple_of(j * T, T), T)
                ar, ai = left[1, 0], left[1, 1]
                br, bi = C[0, at, :], C[1, at, :]
                acc[0, :, at] += dot_nt(ar, br) - dot_nt(ai, bi)
                acc[1, :, at] += dot_nt(ar, bi) + dot_nt(ai, br)
                return 0

            lax.fori_loop(0, N // T, tile, 0)
            cmul(msend, C, Cp)
            for to_x in range(2, NX):
                @pl.when((x >= 1) & (x < to_x))
                def _(to_x=to_x):
                    send_m(to_x).start()

    for c in range(K):
        own[c].wait()
        wait_bytes(recvs[c].at[pl.ds(0, E - 1)], a1r.at[c])

        def energy(t, _, c=c):
            total = None
            for p in range(NP):
                term = phonf[c, mode[t, p]][None] * recvs[c][src[t, p]].astype(F32)
                total = term if total is None else total + term
            sigout[c, t, :, :W] = total[0].astype(BF16)
            sigout[c, t, :, W:] = total[1].astype(BF16)
            return 0

        lax.fori_loop(0, E, energy, 0)
        S[0, c, my_rows, :] = sigout[c, e]
        send_sigma(c)
        if c + 2 < K:
            send_rows(c + 2)
        if c == 0:
            pair_setup()

    def forward_m(i):
        return pltpu.make_async_remote_copy(
            src_ref=mrecv.at[i], dst_ref=mrecv.at[i], send_sem=mfs.at[i], recv_sem=mr.at[i],
            device_id=(e, s + 1 - 2 * core), device_id_type=MESH,
        )

    @pl.when(x >= 1)
    def _():
        @pl.when(core == 0)
        def _():
            left[1 + x] = C[...]

        @pl.when(core == 1)
        def _():
            left[1 + x] = msend[...]

    for i in range(NX - 2):
        @pl.when(x >= i + 2)
        def _(i=i):
            forward_m(i).wait_recv()

            @pl.when(core == 1)
            def _():
                forward_m(i).start()

    def compose(d, _):
        cmul(left.at[1 + x - d], left.at[2 + x - d], mrecv.at[x - d - 1])
        return 0

    lax.fori_loop(1, x, compose, 0)

    def transposes(i, _):
        stack_transposed(2 + i, left.at[2 + i])
        return 0

    lax.fori_loop(0, x, transposes, 0)

    row_at = lax.broadcasted_iota(jnp.int32, (N, 2 * W), 0)
    lane_at = lax.broadcasted_iota(jnp.int32, (N, 2 * W), 1)

    def absorb_sigma(slot, c, slab_at):
        active = jnp.where(slab_at < act[0], 1.0, 0.0).astype(F32)
        on_diagonal = (row_at == lane_at + c * W) & (lane_at < W)
        chunk = S[slot, c].astype(F32) * active + jnp.where(on_diagonal, off[0], 0.0)
        absorb(slot, c, chunk.astype(BF16))

    def to_core1(c):
        return pltpu.make_async_remote_copy(
            src_ref=S.at[0, c], dst_ref=S.at[1, c], send_sem=sps.at[c], recv_sem=spr.at[c],
            device_id=(e, s + 1 - 2 * core), device_id_type=MESH,
        )

    def scatter(c, _):
        wait_bytes(S.at[0, c, pl.ds(0, N - R), :], a2r.at[c])

        @pl.when(core == 0)
        def _():
            to_core1(c).start()

        absorb_sigma(0, c, s)

        @pl.when(core == 1)
        def _():
            to_core1(c).wait_recv()
            absorb_sigma(1, c, s - 1)

        return 0

    lax.fori_loop(0, K, scatter, 0)

    def send_p(c, to_x, way):
        return pltpu.make_async_remote_copy(
            src_ref=psend.at[c], dst_ref=S.at[2 + x, c], send_sem=pss.at[way, c], recv_sem=prc.at[x, c],
            device_id=(e, 2 * to_x + 1), device_id_type=MESH,
        )

    @pl.when((core == 1) & (x < NX - 1))
    def _():
        def fill(c, _):
            at = pl.ds(pl.multiple_of(c * W, W), W)
            psend[c, :, :W] = acc[0, :, at].astype(BF16)
            psend[c, :, W:] = acc[1, :, at].astype(BF16)
            return 0

        lax.fori_loop(0, K, fill, 0)

        def go(c, _):
            send_p(c, x + 1, 0).start()

            @pl.when(x == 0)
            def _():
                send_p(c, NX - 1, 1).start()

            return 0

        lax.fori_loop(0, K, go, 0)

    def forward_p(i, c):
        return pltpu.make_async_remote_copy(
            src_ref=S.at[2 + i, c], dst_ref=S.at[2 + i, c], send_sem=psf.at[i, c], recv_sem=prc.at[i, c],
            device_id=(e, s + 1 - 2 * core), device_id_type=MESH,
        )

    def relay_p(i, c):
        return pltpu.make_async_remote_copy(
            src_ref=S.at[2 + i, c], dst_ref=S.at[2 + i, c], send_sem=prl.at[c], recv_sem=prc.at[i, c],
            device_id=(e, 2 * (5 - x) + 1), device_id_type=MESH,
        )

    def take(i, c):
        forward_p(i, c).wait_recv()

        @pl.when(core == 1)
        def _():
            @pl.when(((x == 3) & (i == 0)) | ((x == 2) & (i == 1)))
            def _():
                relay_p(i, c).start()

            forward_p(i, c).start()

        absorb(2 + i, c, S[2 + i, c])

    def arrivals(t, _):
        late = (x // 3) * (t // (2 * K))
        pairs = (x + 1) // 2 - (1 - x // 2)
        i1, c1 = 0, t
        i2, c2 = 1 - t % 2, t // 2
        i3 = (1 - late) * 2 * (t % 2) + late
        c3 = (1 - late) * (t // 2) + late * (t - 2 * K)
        is1 = (x % 2) * (1 - x // 2)
        is2 = (x // 2) * (1 - x % 2)
        is3 = x // 3
        i = is1 * i1 + is2 * i2 + is3 * i3
        c = is1 * c1 + is2 * c2 + is3 * c3
        take(i, c)
        return 0

    lax.fori_loop(0, K * x, arrivals, 0)

    eye = lax.broadcasted_iota(jnp.int32, (W, W), 0) == lax.broadcasted_iota(jnp.int32, (W, W), 1)

    def write(c):
        return pltpu.make_async_copy(ostage.at[c], out.at[0, 0, :, :, pl.ds(c * W, W)], out_sem.at[c])

    for c in range(K):
        ostage[c, 0] = acc[0, :, c * W:(c + 1) * W].astype(BF16)
        im = acc[1, :, c * W:(c + 1) * W].astype(BF16)
        ostage[c, 1] = im
        square = im[c * W:(c + 1) * W, :].astype(F32)
        diagonal = jnp.sum(jnp.where(eye, square, 0.0), axis=0, keepdims=True)
        dsend[:, c * W:(c + 1) * W] = -occ[0] * diagonal

    drecv[e] = dsend[...]

    def send_density(k, _):
        pltpu.make_async_remote_copy(
            src_ref=dsend, dst_ref=drecv.at[e], send_sem=ds, recv_sem=dr, device_id=(peer_of(k), s), device_id_type=MESH
        ).start()
        return 0

    lax.fori_loop(1, E, send_density, 0)
    for c in range(K):
        write(c).start()

    wait_bytes(drecv.at[pl.ds(0, E - 1)], dr)
    dens[...] = jnp.sum(drecv[...], axis=0)

    wait_bytes(drecv.at[pl.ds(0, E - 1)], ds)
    for c in range(K):
        write(c).wait()

    for c in range(K):
        wait_bytes(recvs[c].at[pl.ds(0, E - 1)], a1s.at[c])

    def drain(c, _):
        wait_bytes(sigout.at[c, pl.ds(0, E - 1)], a2s.at[c])

        @pl.when(core == 0)
        def _():
            to_core1(c).wait_send()

        @pl.when((core == 1) & (x < NX - 1))
        def _():
            send_p(c, x + 1, 0).wait_send()

            @pl.when(x == 0)
            def _():
                send_p(c, NX - 1, 1).wait_send()

        @pl.when((core == 1) & (x >= 2))
        def _():
            relay_p(0, c).wait_send()

        @pl.when(core == 1)
        def _():
            def one(i, _):
                forward_p(i, c).wait_send()
                return 0

            lax.fori_loop(0, x, one, 0)

        return 0

    lax.fori_loop(0, K, drain, 0)

    @pl.when(core == 0)
    def _():
        to_partner.wait_send()

    @pl.when(core == 1)
    def _():
        for to_x in range(2, NX):
            @pl.when((x >= 1) & (x < to_x))
            def _(to_x=to_x):
                send_m(to_x).wait_send()
        for i in range(NX - 2):
            @pl.when(x >= i + 2)
            def _(i=i):
                forward_m(i).wait_send()


def solution(mesh):
    E, NS = mesh.shape["energy"], mesh.shape["slab"]
    NY = min(4, E)

    def local(green, inv, coup, phon, off, occ, src, mode, act):
        N = coup.shape[0]
        K = CHUNKS
        R, W, NX = N // E, N // K, NS // 2
        NM, NP = phon.shape[0], src.shape[1]
        sizes = (E, NS, N, K, NM, NP, NY)
        anywhere = pl.BlockSpec(memory_space=pl.ANY)
        smem = pl.BlockSpec(memory_space=pltpu.SMEM)
        vmem = pl.BlockSpec(memory_space=pltpu.VMEM)
        dma = pltpu.SemaphoreType.DMA
        matrix = pltpu.VMEM((2, N, N), BF16)
        scratch = [
            *[pltpu.VMEM((E, 2, R, W), BF16) for _ in range(K)],
            pltpu.VMEM((K, E, R, 2 * W), BF16),
            pltpu.VMEM((1 + NX, K, N, 2 * W), BF16),
            pltpu.VMEM((K, N, 2 * W), BF16),
            pltpu.VMEM((1 + NX, 2, N, N), BF16),
            pltpu.VMEM((1 + NX, K, 2 * W, N), BF16),
            pltpu.VMEM((1 + NX, K, 2 * W, N), BF16),
            matrix,
            pltpu.VMEM((N, N), BF16),
            pltpu.VMEM((K, NM, R, W), F32),
            matrix,
            matrix,
            matrix,
            pltpu.VMEM((NX - 2, 2, N, N), BF16),
            matrix,
            pltpu.VMEM((2, N, N), F32),
            pltpu.VMEM((K, 2, N, W), BF16),
            pltpu.VMEM((1, N), F32),
            pltpu.VMEM((E, 1, N), F32),
            dma((2,)), dma((K,)),
            dma((K,)), dma((K,)), dma((K,)), dma((K,)),
            dma, dma,
            dma((NX,)), dma((NX - 2,)), dma((NX - 2,)),
            dma((K,)), dma((K,)),
            dma((2, K)), dma((NX - 1, K)), dma((K,)), dma((NX - 1, K)),
            dma((K,)), dma, dma,
        ]
        return pl.pallas_call(
            functools.partial(kernel, sizes),
            out_shape=(
                jax.ShapeDtypeStruct((1, 1, 2, N, N), BF16),
                jax.ShapeDtypeStruct((1, N), F32),
            ),
            in_specs=[anywhere, anywhere, anywhere, vmem, smem, smem, smem, smem, smem],
            out_specs=(anywhere, vmem),
            scratch_shapes=scratch,
            compiler_params=pltpu.CompilerParams(
                collective_id=0, has_side_effects=True, vmem_limit_bytes=60 * 1024 * 1024
            ),
            name="born",
        )(green, inv, coup, phon, off, occ, src, mode, act)

    in_specs = (
        P("energy", "slab", None, None, None),
        P("slab", None, None, None),
        P(),
        P(None, "energy", None),
        P("energy"),
        P("energy"),
        P(),
        P(),
        P("energy"),
    )
    out_specs = (P("energy", "slab", None, None, None), P("slab", None))
    return jax.shard_map(local, mesh=mesh, in_specs=in_specs, out_specs=out_specs, check_vma=False)
```

```python
import functools

import jax
import jax.numpy as jnp
from jax import lax
from jax.experimental import pallas as pl
from jax.experimental.pallas import tpu as pltpu
from jax.sharding import PartitionSpec as P

MESH = pl.DeviceIdType.MESH
CHUNKS = 4
BF16 = jnp.bfloat16
F32 = jnp.float32


def dot(a, b):
    return jnp.dot(a, b, preferred_element_type=F32)


def dot_nt(a, b):
    return lax.dot_general(a, b, (((1,), (1,)), ((), ())), preferred_element_type=F32)


def kernel(
    sizes,
    green, inv, coup, phon, off, occ, src, mode, act,
    out, dens, *scratch,
):
    E, NS, N, K, NM, NP, NY = sizes
    recvs = scratch[:K]
    (
        sigout, S, psend, left, QR, QI, prev, V, phonf, C, Cp, tmp, mrecv, msend, acc, ostage, dsend, drecv,
        load_sem, own_sem, a1s, a1r, a2s, a2r, prs, prr, ms, mr, mfs, sps, spr, pss, psf, prl, prc, out_sem, ds, dr,
    ) = scratch[K:]
    NZ = E // NY
    R = N // E
    W = N // K
    NX = NS // 2
    e = lax.axis_index("energy")
    s = lax.axis_index("slab")
    z, y = e // NY, e % NY
    x, core = s // 2, s % 2
    T = min(256, N)

    def peer_of(k):
        i = k % NZ
        j = k // NZ
        dz = (i % 2) * ((i + 1) // 2) + (1 - i % 2) * ((NZ - i // 2) % NZ)
        return ((z + dz) % NZ) * NY + (y + j) % NY

    barrier = pltpu.get_barrier_semaphore()

    def greet(k, _):
        pl.semaphore_signal(barrier, inc=1, device_id=(peer_of(k), s), device_id_type=MESH)
        return 0

    lax.fori_loop(1, E, greet, 0)

    def greet_x(k, _):
        pl.semaphore_signal(barrier, inc=1, device_id=(e, (s + k) % NS), device_id_type=MESH)
        return 0

    lax.fori_loop(1, NS, greet_x, 0)

    load_inv = pltpu.make_async_copy(inv.at[0], left.at[0], load_sem.at[0])
    load_inv.start()
    load_v = pltpu.make_async_copy(coup, V, load_sem.at[1])
    load_v.start()
    my_rows = pl.ds(pl.multiple_of(e * R, R), R)
    own = []
    for c in range(K):
        own.append(
            pltpu.make_async_copy(green.at[0, 0, :, my_rows, pl.ds(c * W, W)], recvs[c].at[e], own_sem.at[c])
        )
        own[-1].start()
    for c in range(K):
        phonf[c] = phon[:, :, c * W:(c + 1) * W].astype(F32)

    pl.semaphore_wait(barrier, E - 1 + NS - 1)

    def send_rows(c):
        def one(k, _):
            p = peer_of(k)
            pltpu.make_async_remote_copy(
                src_ref=green.at[0, 0, :, pl.ds(pl.multiple_of(p * R, R), R), pl.ds(pl.multiple_of(c * W, W), W)],
                dst_ref=recvs[c].at[e],
                send_sem=a1s.at[c],
                recv_sem=a1r.at[c],
                device_id=(p, s),
                device_id_type=MESH,
            ).start()
            return 0

        lax.fori_loop(1, E, one, 0)

    def send_sigma(c):
        def one(k, _):
            p = peer_of(k)
            pltpu.make_async_remote_copy(
                src_ref=sigout.at[c, p],
                dst_ref=S.at[0, c, my_rows, :],
                send_sem=a2s.at[c],
                recv_sem=a2r.at[c],
                device_id=(p, s),
                device_id_type=MESH,
            ).start()
            return 0

        lax.fori_loop(1, E, one, 0)

    def wait_bytes(ref, sem):
        pltpu.make_async_copy(ref, ref, sem).wait()

    send_rows(0)
    send_rows(1)
    to_partner = pltpu.make_async_remote_copy(
        src_ref=inv.at[0], dst_ref=prev, send_sem=prs, recv_sem=prr, device_id=(e, s + 1 - 2 * core), device_id_type=MESH
    )

    @pl.when(core == 0)
    def _():
        to_partner.start()

    def cmul(dst, a, b, nt=False):
        def tile(j, _):
            at = pl.ds(pl.multiple_of(j * T, T), T)
            if nt:
                br, bi, mm = b[0, at, :], b[1, at, :], dot_nt
            else:
                br, bi, mm = b[0, :, at], b[1, :, at], dot
            ar, ai = a[0], a[1]
            dst[0, :, at] = (mm(ar, br) - mm(ai, bi)).astype(dst.dtype)
            dst[1, :, at] = (mm(ar, bi) + mm(ai, br)).astype(dst.dtype)
            return 0

        lax.fori_loop(0, N // T, tile, 0)

    def stack_rows(slot, q):
        def one(c, _):
            at = pl.ds(pl.multiple_of(c * W, W), W)
            QR[slot, c, :W, :] = q[0, at, :]
            QR[slot, c, W:, :] = q[1, at, :]
            QI[slot, c, :W, :] = q[1, at, :]
            QI[slot, c, W:, :] = q[0, at, :]
            return 0

        lax.fori_loop(0, K, one, 0)

    def stack_transposed(slot, q):
        def one(c, _):
            at = pl.ds(pl.multiple_of(c * W, W), W)
            tr = q[0, :, at].astype(F32).T.astype(BF16)
            ti = q[1, :, at].astype(F32).T.astype(BF16)
            QR[slot, c, :W, :] = tr
            QR[slot, c, W:, :] = ti
            QI[slot, c, :W, :] = ti
            QI[slot, c, W:, :] = tr
            return 0

        lax.fori_loop(0, K, one, 0)

    def couple(dst, a):
        def one(k, _):
            dst[k] = dot(a[k], V[...]).astype(BF16)
            return 0

        lax.fori_loop(0, 2, one, 0)

    def absorb(slot, c, chunk):
        u = dot(left[slot, 0], chunk)
        v = dot(left[slot, 1], chunk)
        hr = (u[:, :W] - v[:, W:]).astype(BF16)
        hi = (u[:, W:] + v[:, :W]).astype(BF16)
        acc[0] += dot(jnp.concatenate((hr, -hi), axis=1), QR[slot, c])
        acc[1] += dot(jnp.concatenate((hr, hi), axis=1), QI[slot, c])

    load_inv.wait()
    load_v.wait()
    couple(C, left.at[0])
    stack_rows(0, left.at[0])
    acc[...] = left[0].astype(F32)

    def send_m(to_x):
        return pltpu.make_async_remote_copy(
            src_ref=msend, dst_ref=mrecv.at[x - 1], send_sem=ms.at[to_x], recv_sem=mr.at[x - 1],
            device_id=(e, 2 * to_x + 1), device_id_type=MESH,
        )

    def pair_setup():
        @pl.when(core == 1)
        def _():
            to_partner.wait_recv()
            couple(Cp, prev)
            cmul(left.at[1], C, prev)
            cmul(tmp, prev, C, nt=True)
            stack_rows(1, tmp)

            def tile(j, _):
                at = pl.ds(pl.multiple_of(j * T, T), T)
                ar, ai = left[1, 0], left[1, 1]
                br, bi = C[0, at, :], C[1, at, :]
                acc[0, :, at] += dot_nt(ar, br) - dot_nt(ai, bi)
                acc[1, :, at] += dot_nt(ar, bi) + dot_nt(ai, br)
                return 0

            lax.fori_loop(0, N // T, tile, 0)
            cmul(msend, C, Cp)
            for to_x in range(2, NX):
                @pl.when((x >= 1) & (x < to_x))
                def _(to_x=to_x):
                    send_m(to_x).start()

    for c in range(K):
        own[c].wait()
        wait_bytes(recvs[c].at[pl.ds(0, E - 1)], a1r.at[c])

        def energy(t, _, c=c):
            total = None
            for p in range(NP):
                term = phonf[c, mode[t, p]][None] * recvs[c][src[t, p]].astype(F32)
                total = term if total is None else total + term
            sigout[c, t, :, :W] = total[0].astype(BF16)
            sigout[c, t, :, W:] = total[1].astype(BF16)
            return 0

        lax.fori_loop(0, E, energy, 0)
        S[0, c, my_rows, :] = sigout[c, e]
        send_sigma(c)
        if c + 2 < K:
            send_rows(c + 2)
        if c == 0:
            pair_setup()

    def forward_m(i):
        return pltpu.make_async_remote_copy(
            src_ref=mrecv.at[i], dst_ref=mrecv.at[i], send_sem=mfs.at[i], recv_sem=mr.at[i],
            device_id=(e, s + 1 - 2 * core), device_id_type=MESH,
        )

    @pl.when(x >= 1)
    def _():
        @pl.when(core == 0)
        def _():
            left[1 + x] = C[...]

        @pl.when(core == 1)
        def _():
            left[1 + x] = msend[...]

    for i in range(NX - 2):
        @pl.when(x >= i + 2)
        def _(i=i):
            forward_m(i).wait_recv()

            @pl.when(core == 1)
            def _():
                forward_m(i).start()

    def compose(d, _):
        cmul(left.at[1 + x - d], left.at[2 + x - d], mrecv.at[x - d - 1])
        return 0

    lax.fori_loop(1, x, compose, 0)

    def transposes(i, _):
        stack_transposed(2 + i, left.at[2 + i])
        return 0

    lax.fori_loop(0, x, transposes, 0)

    row_at = lax.broadcasted_iota(jnp.int32, (N, 2 * W), 0)
    lane_at = lax.broadcasted_iota(jnp.int32, (N, 2 * W), 1)

    def absorb_sigma(slot, c, slab_at):
        active = jnp.where(slab_at < act[0], 1.0, 0.0).astype(F32)
        on_diagonal = (row_at == lane_at + c * W) & (lane_at < W)
        chunk = S[slot, c].astype(F32) * active + jnp.where(on_diagonal, off[0], 0.0)
        absorb(slot, c, chunk.astype(BF16))

    def to_core1(c):
        return pltpu.make_async_remote_copy(
            src_ref=S.at[0, c], dst_ref=S.at[1, c], send_sem=sps.at[c], recv_sem=spr.at[c],
            device_id=(e, s + 1 - 2 * core), device_id_type=MESH,
        )

    def scatter(c, _):
        wait_bytes(S.at[0, c, pl.ds(0, N - R), :], a2r.at[c])

        @pl.when(core == 0)
        def _():
            to_core1(c).start()

        absorb_sigma(0, c, s)

        @pl.when(core == 1)
        def _():
            to_core1(c).wait_recv()
            absorb_sigma(1, c, s - 1)

        return 0

    lax.fori_loop(0, K, scatter, 0)

    def send_p(c, to_x, way):
        return pltpu.make_async_remote_copy(
            src_ref=psend.at[c], dst_ref=S.at[2 + x, c], send_sem=pss.at[way, c], recv_sem=prc.at[x, c],
            device_id=(e, 2 * to_x + 1), device_id_type=MESH,
        )

    @pl.when((core == 1) & (x < NX - 1))
    def _():
        def fill(c, _):
            at = pl.ds(pl.multiple_of(c * W, W), W)
            psend[c, :, :W] = acc[0, :, at].astype(BF16)
            psend[c, :, W:] = acc[1, :, at].astype(BF16)
            return 0

        lax.fori_loop(0, K, fill, 0)

        def go(c, _):
            send_p(c, x + 1, 0).start()

            @pl.when(x == 0)
            def _():
                send_p(c, NX - 1, 1).start()

            @pl.when((x == 1) & (c % 2 == 1))
            def _():
                send_p(c, 0, 1).start()

            return 0

        lax.fori_loop(0, K, go, 0)

    def forward_p(i, c):
        return pltpu.make_async_remote_copy(
            src_ref=S.at[2 + i, c], dst_ref=S.at[2 + i, c], send_sem=psf.at[i, c], recv_sem=prc.at[i, c],
            device_id=(e, s + 1 - 2 * core), device_id_type=MESH,
        )

    def relay_p(i, c):
        return pltpu.make_async_remote_copy(
            src_ref=S.at[2 + i, c], dst_ref=S.at[2 + i, c], send_sem=prl.at[c], recv_sem=prc.at[i, c],
            device_id=(e, 2 * (5 - x) + 1), device_id_type=MESH,
        )

    def relay_back(c):
        return pltpu.make_async_remote_copy(
            src_ref=S.at[3, c], dst_ref=S.at[3, c], send_sem=prl.at[c], recv_sem=prc.at[1, c],
            device_id=(e, 2 * NX - 1), device_id_type=MESH,
        )

    @pl.when((core == 1) & (x == 0))
    def _():
        def back(h, _):
            relay_back(2 * h + 1).wait_recv()
            relay_back(2 * h + 1).start()
            return 0

        lax.fori_loop(0, K // 2, back, 0)

    def take(i, c):
        forward_p(i, c).wait_recv()

        @pl.when(core == 1)
        def _():
            @pl.when(((x == 3) & (i == 0)) | ((x == 2) & (i == 1) & (c % 2 == 0)))
            def _():
                relay_p(i, c).start()

            forward_p(i, c).start()

        absorb(2 + i, c, S[2 + i, c])

    def arrivals(t, _):
        late = (x // 3) * (t // (2 * K))
        pairs = (x + 1) // 2 - (1 - x // 2)
        i1, c1 = 0, t
        i2, c2 = 1 - t % 2, t // 2
        i3 = (1 - late) * 2 * (t % 2) + late
        c3 = (1 - late) * (t // 2) + late * (t - 2 * K)
        is1 = (x % 2) * (1 - x // 2)
        is2 = (x // 2) * (1 - x % 2)
        is3 = x // 3
        i = is1 * i1 + is2 * i2 + is3 * i3
        c = is1 * c1 + is2 * c2 + is3 * c3
        take(i, c)
        return 0

    lax.fori_loop(0, K * x, arrivals, 0)

    eye = lax.broadcasted_iota(jnp.int32, (W, W), 0) == lax.broadcasted_iota(jnp.int32, (W, W), 1)

    def write(c):
        return pltpu.make_async_copy(ostage.at[c], out.at[0, 0, :, :, pl.ds(c * W, W)], out_sem.at[c])

    for c in range(K):
        square = acc[1, c * W:(c + 1) * W, c * W:(c + 1) * W].astype(BF16).astype(F32)
        diagonal = jnp.sum(jnp.where(eye, square, 0.0), axis=0, keepdims=True)
        dsend[:, c * W:(c + 1) * W] = -occ[0] * diagonal

    drecv[e] = dsend[...]

    def send_density(k, _):
        pltpu.make_async_remote_copy(
            src_ref=dsend, dst_ref=drecv.at[e], send_sem=ds, recv_sem=dr, device_id=(peer_of(k), s), device_id_type=MESH
        ).start()
        return 0

    lax.fori_loop(1, E, send_density, 0)
    for c in range(K):
        ostage[c, 0] = acc[0, :, c * W:(c + 1) * W].astype(BF16)
        ostage[c, 1] = acc[1, :, c * W:(c + 1) * W].astype(BF16)
        write(c).start()

    wait_bytes(drecv.at[pl.ds(0, E - 1)], dr)
    dens[...] = jnp.sum(drecv[...], axis=0)

    wait_bytes(drecv.at[pl.ds(0, E - 1)], ds)
    for c in range(K):
        write(c).wait()

    for c in range(K):
        wait_bytes(recvs[c].at[pl.ds(0, E - 1)], a1s.at[c])

    def drain(c, _):
        wait_bytes(sigout.at[c, pl.ds(0, E - 1)], a2s.at[c])

        @pl.when(core == 0)
        def _():
            to_core1(c).wait_send()

        @pl.when((core == 1) & (x < NX - 1))
        def _():
            send_p(c, x + 1, 0).wait_send()

            @pl.when(x == 0)
            def _():
                send_p(c, NX - 1, 1).wait_send()

            @pl.when((x == 1) & (c % 2 == 1))
            def _():
                send_p(c, 0, 1).wait_send()

        @pl.when((core == 1) & ((x == 3) | ((x == 2) & (c % 2 == 0))))
        def _():
            relay_p(0, c).wait_send()

        @pl.when((core == 1) & (x == 0) & (c % 2 == 1))
        def _():
            relay_back(c).wait_send()

        @pl.when(core == 1)
        def _():
            def one(i, _):
                forward_p(i, c).wait_send()
                return 0

            lax.fori_loop(0, x, one, 0)

        return 0

    lax.fori_loop(0, K, drain, 0)

    @pl.when(core == 0)
    def _():
        to_partner.wait_send()

    @pl.when(core == 1)
    def _():
        for to_x in range(2, NX):
            @pl.when((x >= 1) & (x < to_x))
            def _(to_x=to_x):
                send_m(to_x).wait_send()
        for i in range(NX - 2):
            @pl.when(x >= i + 2)
            def _(i=i):
                forward_m(i).wait_send()


def solution(mesh):
    E, NS = mesh.shape["energy"], mesh.shape["slab"]
    NY = min(4, E)

    def local(green, inv, coup, phon, off, occ, src, mode, act):
        N = coup.shape[0]
        K = CHUNKS
        R, W, NX = N // E, N // K, NS // 2
        NM, NP = phon.shape[0], src.shape[1]
        sizes = (E, NS, N, K, NM, NP, NY)
        anywhere = pl.BlockSpec(memory_space=pl.ANY)
        smem = pl.BlockSpec(memory_space=pltpu.SMEM)
        vmem = pl.BlockSpec(memory_space=pltpu.VMEM)
        dma = pltpu.SemaphoreType.DMA
        matrix = pltpu.VMEM((2, N, N), BF16)
        scratch = [
            *[pltpu.VMEM((E, 2, R, W), BF16) for _ in range(K)],
            pltpu.VMEM((K, E, R, 2 * W), BF16),
            pltpu.VMEM((1 + NX, K, N, 2 * W), BF16),
            pltpu.VMEM((K, N, 2 * W), BF16),
            pltpu.VMEM((1 + NX, 2, N, N), BF16),
            pltpu.VMEM((1 + NX, K, 2 * W, N), BF16),
            pltpu.VMEM((1 + NX, K, 2 * W, N), BF16),
            matrix,
            pltpu.VMEM((N, N), BF16),
            pltpu.VMEM((K, NM, R, W), F32),
            matrix,
            matrix,
            matrix,
            pltpu.VMEM((NX - 2, 2, N, N), BF16),
            matrix,
            pltpu.VMEM((2, N, N), F32),
            pltpu.VMEM((K, 2, N, W), BF16),
            pltpu.VMEM((1, N), F32),
            pltpu.VMEM((E, 1, N), F32),
            dma((2,)), dma((K,)),
            dma((K,)), dma((K,)), dma((K,)), dma((K,)),
            dma, dma,
            dma((NX,)), dma((NX - 2,)), dma((NX - 2,)),
            dma((K,)), dma((K,)),
            dma((2, K)), dma((NX - 1, K)), dma((K,)), dma((NX - 1, K)),
            dma((K,)), dma, dma,
        ]
        return pl.pallas_call(
            functools.partial(kernel, sizes),
            out_shape=(
                jax.ShapeDtypeStruct((1, 1, 2, N, N), BF16),
                jax.ShapeDtypeStruct((1, N), F32),
            ),
            in_specs=[anywhere, anywhere, anywhere, vmem, smem, smem, smem, smem, smem],
            out_specs=(anywhere, vmem),
            scratch_shapes=scratch,
            compiler_params=pltpu.CompilerParams(
                collective_id=0, has_side_effects=True, vmem_limit_bytes=60 * 1024 * 1024
            ),
            name="born",
        )(green, inv, coup, phon, off, occ, src, mode, act)

    in_specs = (
        P("energy", "slab", None, None, None),
        P("slab", None, None, None),
        P(),
        P(None, "energy", None),
        P("energy"),
        P("energy"),
        P(),
        P(),
        P("energy"),
    )
    out_specs = (P("energy", "slab", None, None, None), P("slab", None))
    return jax.shard_map(local, mesh=mesh, in_specs=in_specs, out_specs=out_specs, check_vma=False)
```

```python
import functools

import jax
import jax.numpy as jnp
from jax import lax
from jax.experimental import pallas as pl
from jax.experimental.pallas import tpu as pltpu
from jax.sharding import PartitionSpec as P

MESH = pl.DeviceIdType.MESH
CHUNKS = 4
BF16 = jnp.bfloat16
F32 = jnp.float32


def dot(a, b):
    return jnp.dot(a, b, preferred_element_type=F32)


def dot_nt(a, b):
    return lax.dot_general(a, b, (((1,), (1,)), ((), ())), preferred_element_type=F32)


def kernel(
    sizes,
    green, inv, coup, phon, off, occ, src, mode, act,
    out, dens, *scratch,
):
    E, NS, N, K, NM, NP, NY = sizes
    recvs = scratch[:K]
    (
        sigout, S, psend, left, QR, QI, prev, V, phonf, C, Cp, tmp, mrecv, msend, acc, ostage, dsend, drecv,
        load_sem, own_sem, a1s, a1r, a2s, a2r, prs, prr, ms, mr, mfs, sps, spr, pss, psf, prl, prc, out_sem, ds, dr,
    ) = scratch[K:]
    NZ = E // NY
    R = N // E
    W = N // K
    NX = NS // 2
    e = lax.axis_index("energy")
    s = lax.axis_index("slab")
    z, y = e // NY, e % NY
    x, core = s // 2, s % 2
    T = min(256, N)

    def peer_of(k):
        i = (E - k) // NY
        j = (E - k) % NY
        dz = (i % 2) * ((i + 1) // 2) + (1 - i % 2) * ((NZ - i // 2) % NZ)
        return ((z + dz) % NZ) * NY + (y + j) % NY

    barrier = pltpu.get_barrier_semaphore()

    def greet(k, _):
        pl.semaphore_signal(barrier, inc=1, device_id=(peer_of(k), s), device_id_type=MESH)
        return 0

    lax.fori_loop(1, E, greet, 0)

    def greet_x(k, _):
        pl.semaphore_signal(barrier, inc=1, device_id=(e, (s + k) % NS), device_id_type=MESH)
        return 0

    lax.fori_loop(1, NS, greet_x, 0)

    load_inv = pltpu.make_async_copy(inv.at[0], left.at[0], load_sem.at[0])
    load_inv.start()
    load_v = pltpu.make_async_copy(coup, V, load_sem.at[1])
    load_v.start()
    my_rows = pl.ds(pl.multiple_of(e * R, R), R)
    own = []
    for c in range(K):
        own.append(
            pltpu.make_async_copy(green.at[0, 0, :, my_rows, pl.ds(c * W, W)], recvs[c].at[e], own_sem.at[c])
        )
        own[-1].start()
    for c in range(K):
        phonf[c] = phon[:, :, c * W:(c + 1) * W].astype(F32)

    pl.semaphore_wait(barrier, E - 1 + NS - 1)

    def send_rows(c):
        def one(k, _):
            p = peer_of(k)
            pltpu.make_async_remote_copy(
                src_ref=green.at[0, 0, :, pl.ds(pl.multiple_of(p * R, R), R), pl.ds(pl.multiple_of(c * W, W), W)],
                dst_ref=recvs[c].at[e],
                send_sem=a1s.at[c],
                recv_sem=a1r.at[c],
                device_id=(p, s),
                device_id_type=MESH,
            ).start()
            return 0

        lax.fori_loop(1, E, one, 0)

    def send_sigma(c):
        def one(k, _):
            p = peer_of(k)
            pltpu.make_async_remote_copy(
                src_ref=sigout.at[c, p],
                dst_ref=S.at[0, c, my_rows, :],
                send_sem=a2s.at[c],
                recv_sem=a2r.at[c],
                device_id=(p, s),
                device_id_type=MESH,
            ).start()
            return 0

        lax.fori_loop(1, E, one, 0)

    def wait_bytes(ref, sem):
        pltpu.make_async_copy(ref, ref, sem).wait()

    send_rows(0)
    send_rows(1)
    to_partner = pltpu.make_async_remote_copy(
        src_ref=inv.at[0], dst_ref=prev, send_sem=prs, recv_sem=prr, device_id=(e, s + 1 - 2 * core), device_id_type=MESH
    )

    @pl.when(core == 0)
    def _():
        to_partner.start()

    def cmul(dst, a, b, nt=False):
        def tile(j, _):
            at = pl.ds(pl.multiple_of(j * T, T), T)
            if nt:
                br, bi, mm = b[0, at, :], b[1, at, :], dot_nt
            else:
                br, bi, mm = b[0, :, at], b[1, :, at], dot
            ar, ai = a[0], a[1]
            dst[0, :, at] = (mm(ar, br) - mm(ai, bi)).astype(dst.dtype)
            dst[1, :, at] = (mm(ar, bi) + mm(ai, br)).astype(dst.dtype)
            return 0

        lax.fori_loop(0, N // T, tile, 0)

    def stack_rows(slot, q):
        def one(c, _):
            at = pl.ds(pl.multiple_of(c * W, W), W)
            QR[slot, c, :W, :] = q[0, at, :]
            QR[slot, c, W:, :] = q[1, at, :]
            QI[slot, c, :W, :] = q[1, at, :]
            QI[slot, c, W:, :] = q[0, at, :]
            return 0

        lax.fori_loop(0, K, one, 0)

    def stack_transposed(slot, q):
        def one(c, _):
            at = pl.ds(pl.multiple_of(c * W, W), W)
            tr = q[0, :, at].astype(F32).T.astype(BF16)
            ti = q[1, :, at].astype(F32).T.astype(BF16)
            QR[slot, c, :W, :] = tr
            QR[slot, c, W:, :] = ti
            QI[slot, c, :W, :] = ti
            QI[slot, c, W:, :] = tr
            return 0

        lax.fori_loop(0, K, one, 0)

    def couple(dst, a):
        def one(k, _):
            dst[k] = dot(a[k], V[...]).astype(BF16)
            return 0

        lax.fori_loop(0, 2, one, 0)

    def absorb(slot, c, chunk):
        u = dot(left[slot, 0], chunk)
        v = dot(left[slot, 1], chunk)
        hr = (u[:, :W] - v[:, W:]).astype(BF16)
        hi = (u[:, W:] + v[:, :W]).astype(BF16)
        acc[0] += dot(jnp.concatenate((hr, -hi), axis=1), QR[slot, c])
        acc[1] += dot(jnp.concatenate((hr, hi), axis=1), QI[slot, c])

    load_inv.wait()
    load_v.wait()
    couple(C, left.at[0])
    stack_rows(0, left.at[0])
    acc[...] = left[0].astype(F32)

    def send_m(to_x):
        return pltpu.make_async_remote_copy(
            src_ref=msend, dst_ref=mrecv.at[x - 1], send_sem=ms.at[to_x], recv_sem=mr.at[x - 1],
            device_id=(e, 2 * to_x + 1), device_id_type=MESH,
        )

    def pair_setup():
        @pl.when(core == 1)
        def _():
            to_partner.wait_recv()
            couple(Cp, prev)
            cmul(left.at[1], C, prev)
            cmul(tmp, prev, C, nt=True)
            stack_rows(1, tmp)

            def tile(j, _):
                at = pl.ds(pl.multiple_of(j * T, T), T)
                ar, ai = left[1, 0], left[1, 1]
                br, bi = C[0, at, :], C[1, at, :]
                acc[0, :, at] += dot_nt(ar, br) - dot_nt(ai, bi)
                acc[1, :, at] += dot_nt(ar, bi) + dot_nt(ai, br)
                return 0

            lax.fori_loop(0, N // T, tile, 0)
            cmul(msend, C, Cp)
            for to_x in range(2, NX):
                @pl.when((x >= 1) & (x < to_x))
                def _(to_x=to_x):
                    send_m(to_x).start()

    for c in range(K):
        own[c].wait()
        wait_bytes(recvs[c].at[pl.ds(0, E - 1)], a1r.at[c])

        def energy(t, _, c=c):
            total = None
            for p in range(NP):
                term = phonf[c, mode[t, p]][None] * recvs[c][src[t, p]].astype(F32)
                total = term if total is None else total + term
            sigout[c, t, :, :W] = total[0].astype(BF16)
            sigout[c, t, :, W:] = total[1].astype(BF16)
            return 0

        lax.fori_loop(0, E, energy, 0)
        S[0, c, my_rows, :] = sigout[c, e]
        send_sigma(c)
        if c + 2 < K:
            send_rows(c + 2)
        if c == 0:
            pair_setup()

    def forward_m(i):
        return pltpu.make_async_remote_copy(
            src_ref=mrecv.at[i], dst_ref=mrecv.at[i], send_sem=mfs.at[i], recv_sem=mr.at[i],
            device_id=(e, s + 1 - 2 * core), device_id_type=MESH,
        )

    @pl.when(x >= 1)
    def _():
        @pl.when(core == 0)
        def _():
            left[1 + x] = C[...]

        @pl.when(core == 1)
        def _():
            left[1 + x] = msend[...]

    for i in range(NX - 2):
        @pl.when(x >= i + 2)
        def _(i=i):
            forward_m(i).wait_recv()

            @pl.when(core == 1)
            def _():
                forward_m(i).start()

    def compose(d, _):
        cmul(left.at[1 + x - d], left.at[2 + x - d], mrecv.at[x - d - 1])
        return 0

    lax.fori_loop(1, x, compose, 0)

    def transposes(i, _):
        stack_transposed(2 + i, left.at[2 + i])
        return 0

    lax.fori_loop(0, x, transposes, 0)

    row_at = lax.broadcasted_iota(jnp.int32, (N, 2 * W), 0)
    lane_at = lax.broadcasted_iota(jnp.int32, (N, 2 * W), 1)

    def absorb_sigma(slot, c, slab_at):
        active = jnp.where(slab_at < act[0], 1.0, 0.0).astype(F32)
        on_diagonal = (row_at == lane_at + c * W) & (lane_at < W)
        chunk = S[slot, c].astype(F32) * active + jnp.where(on_diagonal, off[0], 0.0)
        absorb(slot, c, chunk.astype(BF16))

    def to_core1(c):
        return pltpu.make_async_remote_copy(
            src_ref=S.at[0, c], dst_ref=S.at[1, c], send_sem=sps.at[c], recv_sem=spr.at[c],
            device_id=(e, s + 1 - 2 * core), device_id_type=MESH,
        )

    def scatter(c, _):
        wait_bytes(S.at[0, c, pl.ds(0, N - R), :], a2r.at[c])

        @pl.when(core == 0)
        def _():
            to_core1(c).start()

        absorb_sigma(0, c, s)

        @pl.when(core == 1)
        def _():
            to_core1(c).wait_recv()
            absorb_sigma(1, c, s - 1)

        return 0

    lax.fori_loop(0, K, scatter, 0)

    def send_p(c, to_x, way):
        return pltpu.make_async_remote_copy(
            src_ref=psend.at[c], dst_ref=S.at[2 + x, c], send_sem=pss.at[way, c], recv_sem=prc.at[x, c],
            device_id=(e, 2 * to_x + 1), device_id_type=MESH,
        )

    @pl.when((core == 1) & (x < NX - 1))
    def _():
        def fill(c, _):
            at = pl.ds(pl.multiple_of(c * W, W), W)
            psend[c, :, :W] = acc[0, :, at].astype(BF16)
            psend[c, :, W:] = acc[1, :, at].astype(BF16)
            return 0

        lax.fori_loop(0, K, fill, 0)

        def go(c, _):
            send_p(c, x + 1, 0).start()

            @pl.when(x == 0)
            def _():
                send_p(c, NX - 1, 1).start()

            @pl.when((x == 1) & (c % 2 == 1))
            def _():
                send_p(c, 0, 1).start()

            return 0

        lax.fori_loop(0, K, go, 0)

    def forward_p(i, c):
        return pltpu.make_async_remote_copy(
            src_ref=S.at[2 + i, c], dst_ref=S.at[2 + i, c], send_sem=psf.at[i, c], recv_sem=prc.at[i, c],
            device_id=(e, s + 1 - 2 * core), device_id_type=MESH,
        )

    def relay_p(i, c):
        return pltpu.make_async_remote_copy(
            src_ref=S.at[2 + i, c], dst_ref=S.at[2 + i, c], send_sem=prl.at[c], recv_sem=prc.at[i, c],
            device_id=(e, 2 * (5 - x) + 1), device_id_type=MESH,
        )

    def relay_back(c):
        return pltpu.make_async_remote_copy(
            src_ref=S.at[3, c], dst_ref=S.at[3, c], send_sem=prl.at[c], recv_sem=prc.at[1, c],
            device_id=(e, 2 * NX - 1), device_id_type=MESH,
        )

    @pl.when((core == 1) & (x == 0))
    def _():
        def back(h, _):
            relay_back(2 * h + 1).wait_recv()
            relay_back(2 * h + 1).start()
            return 0

        lax.fori_loop(0, K // 2, back, 0)

    def take(i, c):
        forward_p(i, c).wait_recv()

        @pl.when(core == 1)
        def _():
            @pl.when(((x == 3) & (i == 0)) | ((x == 2) & (i == 1) & (c % 2 == 0)))
            def _():
                relay_p(i, c).start()

            forward_p(i, c).start()

        absorb(2 + i, c, S[2 + i, c])

    def arrivals(t, _):
        late = (x // 3) * (t // (2 * K))
        pairs = (x + 1) // 2 - (1 - x // 2)
        i1, c1 = 0, t
        i2, c2 = 1 - t % 2, t // 2
        i3 = (1 - late) * 2 * (t % 2) + late
        c3 = (1 - late) * (t // 2) + late * (t - 2 * K)
        is1 = (x % 2) * (1 - x // 2)
        is2 = (x // 2) * (1 - x % 2)
        is3 = x // 3
        i = is1 * i1 + is2 * i2 + is3 * i3
        c = is1 * c1 + is2 * c2 + is3 * c3
        take(i, c)
        return 0

    lax.fori_loop(0, K * x, arrivals, 0)

    eye = lax.broadcasted_iota(jnp.int32, (W, W), 0) == lax.broadcasted_iota(jnp.int32, (W, W), 1)

    def write(c):
        return pltpu.make_async_copy(ostage.at[c], out.at[0, 0, :, :, pl.ds(c * W, W)], out_sem.at[c])

    for c in range(K):
        square = acc[1, c * W:(c + 1) * W, c * W:(c + 1) * W].astype(BF16).astype(F32)
        diagonal = jnp.sum(jnp.where(eye, square, 0.0), axis=0, keepdims=True)
        dsend[:, c * W:(c + 1) * W] = -occ[0] * diagonal

    drecv[e] = dsend[...]

    def send_density(k, _):
        pltpu.make_async_remote_copy(
            src_ref=dsend, dst_ref=drecv.at[e], send_sem=ds, recv_sem=dr, device_id=(peer_of(k), s), device_id_type=MESH
        ).start()
        return 0

    lax.fori_loop(1, E, send_density, 0)
    for c in range(K):
        ostage[c, 0] = acc[0, :, c * W:(c + 1) * W].astype(BF16)
        ostage[c, 1] = acc[1, :, c * W:(c + 1) * W].astype(BF16)
        write(c).start()

    wait_bytes(drecv.at[pl.ds(0, E - 1)], dr)
    dens[...] = jnp.sum(drecv[...], axis=0)

    wait_bytes(drecv.at[pl.ds(0, E - 1)], ds)
    for c in range(K):
        write(c).wait()

    for c in range(K):
        wait_bytes(recvs[c].at[pl.ds(0, E - 1)], a1s.at[c])

    def drain(c, _):
        wait_bytes(sigout.at[c, pl.ds(0, E - 1)], a2s.at[c])

        @pl.when(core == 0)
        def _():
            to_core1(c).wait_send()

        @pl.when((core == 1) & (x < NX - 1))
        def _():
            send_p(c, x + 1, 0).wait_send()

            @pl.when(x == 0)
            def _():
                send_p(c, NX - 1, 1).wait_send()

            @pl.when((x == 1) & (c % 2 == 1))
            def _():
                send_p(c, 0, 1).wait_send()

        @pl.when((core == 1) & ((x == 3) | ((x == 2) & (c % 2 == 0))))
        def _():
            relay_p(0, c).wait_send()

        @pl.when((core == 1) & (x == 0) & (c % 2 == 1))
        def _():
            relay_back(c).wait_send()

        @pl.when(core == 1)
        def _():
            def one(i, _):
                forward_p(i, c).wait_send()
                return 0

            lax.fori_loop(0, x, one, 0)

        return 0

    lax.fori_loop(0, K, drain, 0)

    @pl.when(core == 0)
    def _():
        to_partner.wait_send()

    @pl.when(core == 1)
    def _():
        for to_x in range(2, NX):
            @pl.when((x >= 1) & (x < to_x))
            def _(to_x=to_x):
                send_m(to_x).wait_send()
        for i in range(NX - 2):
            @pl.when(x >= i + 2)
            def _(i=i):
                forward_m(i).wait_send()


def solution(mesh):
    E, NS = mesh.shape["energy"], mesh.shape["slab"]
    NY = min(4, E)

    def local(green, inv, coup, phon, off, occ, src, mode, act):
        N = coup.shape[0]
        K = CHUNKS
        R, W, NX = N // E, N // K, NS // 2
        NM, NP = phon.shape[0], src.shape[1]
        sizes = (E, NS, N, K, NM, NP, NY)
        anywhere = pl.BlockSpec(memory_space=pl.ANY)
        smem = pl.BlockSpec(memory_space=pltpu.SMEM)
        vmem = pl.BlockSpec(memory_space=pltpu.VMEM)
        dma = pltpu.SemaphoreType.DMA
        matrix = pltpu.VMEM((2, N, N), BF16)
        scratch = [
            *[pltpu.VMEM((E, 2, R, W), BF16) for _ in range(K)],
            pltpu.VMEM((K, E, R, 2 * W), BF16),
            pltpu.VMEM((1 + NX, K, N, 2 * W), BF16),
            pltpu.VMEM((K, N, 2 * W), BF16),
            pltpu.VMEM((1 + NX, 2, N, N), BF16),
            pltpu.VMEM((1 + NX, K, 2 * W, N), BF16),
            pltpu.VMEM((1 + NX, K, 2 * W, N), BF16),
            matrix,
            pltpu.VMEM((N, N), BF16),
            pltpu.VMEM((K, NM, R, W), F32),
            matrix,
            matrix,
            matrix,
            pltpu.VMEM((NX - 2, 2, N, N), BF16),
            matrix,
            pltpu.VMEM((2, N, N), F32),
            pltpu.VMEM((K, 2, N, W), BF16),
            pltpu.VMEM((1, N), F32),
            pltpu.VMEM((E, 1, N), F32),
            dma((2,)), dma((K,)),
            dma((K,)), dma((K,)), dma((K,)), dma((K,)),
            dma, dma,
            dma((NX,)), dma((NX - 2,)), dma((NX - 2,)),
            dma((K,)), dma((K,)),
            dma((2, K)), dma((NX - 1, K)), dma((K,)), dma((NX - 1, K)),
            dma((K,)), dma, dma,
        ]
        return pl.pallas_call(
            functools.partial(kernel, sizes),
            out_shape=(
                jax.ShapeDtypeStruct((1, 1, 2, N, N), BF16),
                jax.ShapeDtypeStruct((1, N), F32),
            ),
            in_specs=[anywhere, anywhere, anywhere, vmem, smem, smem, smem, smem, smem],
            out_specs=(anywhere, vmem),
            scratch_shapes=scratch,
            compiler_params=pltpu.CompilerParams(
                collective_id=0, has_side_effects=True, vmem_limit_bytes=60 * 1024 * 1024
            ),
            name="born",
        )(green, inv, coup, phon, off, occ, src, mode, act)

    in_specs = (
        P("energy", "slab", None, None, None),
        P("slab", None, None, None),
        P(),
        P(None, "energy", None),
        P("energy"),
        P("energy"),
        P(),
        P(),
        P("energy"),
    )
    out_specs = (P("energy", "slab", None, None, None), P("slab", None))
    return jax.shard_map(local, mesh=mesh, in_specs=in_specs, out_specs=out_specs, check_vma=False)
```

```python
import functools

import jax
import jax.numpy as jnp
from jax import lax
from jax.experimental import pallas as pl
from jax.experimental.pallas import tpu as pltpu
from jax.sharding import PartitionSpec as P

MESH = pl.DeviceIdType.MESH
CHUNKS = 4
BF16 = jnp.bfloat16
F32 = jnp.float32


def dot(a, b):
    return jnp.dot(a, b, preferred_element_type=F32)


def dot_nt(a, b):
    return lax.dot_general(a, b, (((1,), (1,)), ((), ())), preferred_element_type=F32)


def kernel(
    sizes,
    green, inv, coup, phon, off, occ, pair, act,
    out, dens, *scratch,
):
    E, NS, N, K, NM, NP, NY = sizes
    recvs = scratch[:K]
    (
        sigout, S, psend, left, QR, QI, prev, V, phonf, C, Cp, tmp, mrecv, msend, acc, ostage, dsend, drecv,
        load_sem, own_sem, a1s, a1r, a2s, a2r, prs, prr, ms, mr, mfs, sps, spr, pss, psf, prl, prc, out_sem, ds, dr,
    ) = scratch[K:]
    NZ = E // NY
    R = N // E
    W = N // K
    NX = NS // 2
    e = lax.axis_index("energy")
    s = lax.axis_index("slab")
    z, y = e // NY, e % NY
    x, core = s // 2, s % 2
    T = min(256, N)

    def peer_of(k):
        i = (E - k) // NY
        j = (E - k) % NY
        dz = (i % 2) * ((i + 1) // 2) + (1 - i % 2) * ((NZ - i // 2) % NZ)
        return ((z + dz) % NZ) * NY + (y + j) % NY

    barrier = pltpu.get_barrier_semaphore()

    def greet(k, _):
        pl.semaphore_signal(barrier, inc=1, device_id=(peer_of(k), s), device_id_type=MESH)
        return 0

    lax.fori_loop(1, E, greet, 0)

    def greet_x(k, _):
        pl.semaphore_signal(barrier, inc=1, device_id=(e, (s + k) % NS), device_id_type=MESH)
        return 0

    lax.fori_loop(1, NS, greet_x, 0)

    load_inv = pltpu.make_async_copy(inv.at[0], left.at[0], load_sem.at[0])
    load_inv.start()
    load_v = pltpu.make_async_copy(coup, V, load_sem.at[1])
    load_v.start()
    my_rows = pl.ds(pl.multiple_of(e * R, R), R)
    own = []
    for c in range(K):
        own.append(
            pltpu.make_async_copy(green.at[0, 0, :, my_rows, pl.ds(c * W, W)], recvs[c].at[e], own_sem.at[c])
        )
        own[-1].start()
    for c in range(K):
        phonf[c] = phon[:, :, c * W:(c + 1) * W].astype(F32)

    pl.semaphore_wait(barrier, E - 1 + NS - 1)

    def send_rows(c):
        def one(k, _):
            p = peer_of(k)
            pltpu.make_async_remote_copy(
                src_ref=green.at[0, 0, :, pl.ds(pl.multiple_of(p * R, R), R), pl.ds(pl.multiple_of(c * W, W), W)],
                dst_ref=recvs[c].at[e],
                send_sem=a1s.at[c],
                recv_sem=a1r.at[c],
                device_id=(p, s),
                device_id_type=MESH,
            ).start()
            return 0

        lax.fori_loop(1, E, one, 0)

    def send_sigma(c):
        def one(k, _):
            p = peer_of(k)
            pltpu.make_async_remote_copy(
                src_ref=sigout.at[c, p],
                dst_ref=S.at[0, c, my_rows, :],
                send_sem=a2s.at[c],
                recv_sem=a2r.at[c],
                device_id=(p, s),
                device_id_type=MESH,
            ).start()
            return 0

        lax.fori_loop(1, E, one, 0)

    def wait_bytes(ref, sem):
        pltpu.make_async_copy(ref, ref, sem).wait()

    send_rows(0)
    send_rows(1)
    to_partner = pltpu.make_async_remote_copy(
        src_ref=inv.at[0], dst_ref=prev, send_sem=prs, recv_sem=prr, device_id=(e, s + 1 - 2 * core), device_id_type=MESH
    )

    @pl.when(core == 0)
    def _():
        to_partner.start()

    def cmul(dst, a, b, nt=False):
        def tile(j, _):
            at = pl.ds(pl.multiple_of(j * T, T), T)
            if nt:
                br, bi, mm = b[0, at, :], b[1, at, :], dot_nt
            else:
                br, bi, mm = b[0, :, at], b[1, :, at], dot
            ar, ai = a[0], a[1]
            dst[0, :, at] = (mm(ar, br) - mm(ai, bi)).astype(dst.dtype)
            dst[1, :, at] = (mm(ar, bi) + mm(ai, br)).astype(dst.dtype)
            return 0

        lax.fori_loop(0, N // T, tile, 0)

    def stack_rows(slot, q):
        def one(c, _):
            at = pl.ds(pl.multiple_of(c * W, W), W)
            QR[slot, c, :W, :] = q[0, at, :]
            QR[slot, c, W:, :] = q[1, at, :]
            QI[slot, c, :W, :] = q[1, at, :]
            QI[slot, c, W:, :] = q[0, at, :]
            return 0

        lax.fori_loop(0, K, one, 0)

    def stack_transposed(slot, q):
        def one(c, _):
            at = pl.ds(pl.multiple_of(c * W, W), W)
            tr = q[0, :, at].astype(F32).T.astype(BF16)
            ti = q[1, :, at].astype(F32).T.astype(BF16)
            QR[slot, c, :W, :] = tr
            QR[slot, c, W:, :] = ti
            QI[slot, c, :W, :] = ti
            QI[slot, c, W:, :] = tr
            return 0

        lax.fori_loop(0, K, one, 0)

    def couple(dst, a):
        def one(k, _):
            dst[k] = dot(a[k], V[...]).astype(BF16)
            return 0

        lax.fori_loop(0, 2, one, 0)

    def absorb(slot, c, chunk):
        u = dot(left[slot, 0], chunk)
        v = dot(left[slot, 1], chunk)
        hr = (u[:, :W] - v[:, W:]).astype(BF16)
        hi = (u[:, W:] + v[:, :W]).astype(BF16)
        acc[0] += dot(jnp.concatenate((hr, -hi), axis=1), QR[slot, c])
        acc[1] += dot(jnp.concatenate((hr, hi), axis=1), QI[slot, c])

    load_inv.wait()
    load_v.wait()
    couple(C, left.at[0])
    stack_rows(0, left.at[0])
    acc[...] = left[0].astype(F32)

    def send_m(to_x):
        return pltpu.make_async_remote_copy(
            src_ref=msend, dst_ref=mrecv.at[x - 1], send_sem=ms.at[to_x], recv_sem=mr.at[x - 1],
            device_id=(e, 2 * to_x + 1), device_id_type=MESH,
        )

    def pair_setup():
        @pl.when(core == 1)
        def _():
            to_partner.wait_recv()
            couple(Cp, prev)
            cmul(left.at[1], C, prev)
            cmul(tmp, prev, C, nt=True)
            stack_rows(1, tmp)

            def tile(j, _):
                at = pl.ds(pl.multiple_of(j * T, T), T)
                ar, ai = left[1, 0], left[1, 1]
                br, bi = C[0, at, :], C[1, at, :]
                acc[0, :, at] += dot_nt(ar, br) - dot_nt(ai, bi)
                acc[1, :, at] += dot_nt(ar, bi) + dot_nt(ai, br)
                return 0

            lax.fori_loop(0, N // T, tile, 0)
            cmul(msend, C, Cp)
            for to_x in range(2, NX):
                @pl.when((x >= 1) & (x < to_x))
                def _(to_x=to_x):
                    send_m(to_x).start()

    for c in range(K):
        own[c].wait()
        wait_bytes(recvs[c].at[pl.ds(0, E - 1)], a1r.at[c])

        def energy(t, _, c=c):
            total = None
            for p in range(NP):
                term = phonf[c, pair[t, p] % NM][None] * recvs[c][pair[t, p] // NM].astype(F32)
                total = term if total is None else total + term
            sigout[c, t, :, :W] = total[0].astype(BF16)
            sigout[c, t, :, W:] = total[1].astype(BF16)
            return 0

        lax.fori_loop(0, E, energy, 0)
        S[0, c, my_rows, :] = sigout[c, e]
        send_sigma(c)
        if c + 2 < K:
            send_rows(c + 2)
        if c == 0:
            pair_setup()

    def forward_m(i):
        return pltpu.make_async_remote_copy(
            src_ref=mrecv.at[i], dst_ref=mrecv.at[i], send_sem=mfs.at[i], recv_sem=mr.at[i],
            device_id=(e, s + 1 - 2 * core), device_id_type=MESH,
        )

    @pl.when(x >= 1)
    def _():
        @pl.when(core == 0)
        def _():
            left[1 + x] = C[...]

        @pl.when(core == 1)
        def _():
            left[1 + x] = msend[...]

    for i in range(NX - 2):
        @pl.when(x >= i + 2)
        def _(i=i):
            forward_m(i).wait_recv()

            @pl.when(core == 1)
            def _():
                forward_m(i).start()

    def compose(d, _):
        cmul(left.at[1 + x - d], left.at[2 + x - d], mrecv.at[x - d - 1])
        return 0

    lax.fori_loop(1, x, compose, 0)

    def transposes(i, _):
        stack_transposed(2 + i, left.at[2 + i])
        return 0

    lax.fori_loop(0, x, transposes, 0)

    row_at = lax.broadcasted_iota(jnp.int32, (N, 2 * W), 0)
    lane_at = lax.broadcasted_iota(jnp.int32, (N, 2 * W), 1)

    def absorb_sigma(slot, c, slab_at):
        active = jnp.where(slab_at < act[0], 1.0, 0.0).astype(F32)
        on_diagonal = (row_at == lane_at + c * W) & (lane_at < W)
        chunk = S[slot, c].astype(F32) * active + jnp.where(on_diagonal, off[0], 0.0)
        absorb(slot, c, chunk.astype(BF16))

    def to_core1(c):
        return pltpu.make_async_remote_copy(
            src_ref=S.at[0, c], dst_ref=S.at[1, c], send_sem=sps.at[c], recv_sem=spr.at[c],
            device_id=(e, s + 1 - 2 * core), device_id_type=MESH,
        )

    def scatter(c, _):
        wait_bytes(S.at[0, c, pl.ds(0, N - R), :], a2r.at[c])

        @pl.when(core == 0)
        def _():
            to_core1(c).start()

        absorb_sigma(0, c, s)

        @pl.when(core == 1)
        def _():
            to_core1(c).wait_recv()
            absorb_sigma(1, c, s - 1)

        return 0

    lax.fori_loop(0, K, scatter, 0)

    def send_p(c, to_x, way):
        return pltpu.make_async_remote_copy(
            src_ref=psend.at[c], dst_ref=S.at[2 + x, c], send_sem=pss.at[way, c], recv_sem=prc.at[x, c],
            device_id=(e, 2 * to_x + 1), device_id_type=MESH,
        )

    @pl.when((core == 1) & (x < NX - 1))
    def _():
        def fill(c, _):
            at = pl.ds(pl.multiple_of(c * W, W), W)
            psend[c, :, :W] = acc[0, :, at].astype(BF16)
            psend[c, :, W:] = acc[1, :, at].astype(BF16)
            return 0

        lax.fori_loop(0, K, fill, 0)

        def go(c, _):
            send_p(c, x + 1, 0).start()

            @pl.when(x == 0)
            def _():
                send_p(c, NX - 1, 1).start()

            @pl.when((x == 1) & (c % 2 == 1))
            def _():
                send_p(c, 0, 1).start()

            return 0

        lax.fori_loop(0, K, go, 0)

    def forward_p(i, c):
        return pltpu.make_async_remote_copy(
            src_ref=S.at[2 + i, c], dst_ref=S.at[2 + i, c], send_sem=psf.at[i, c], recv_sem=prc.at[i, c],
            device_id=(e, s + 1 - 2 * core), device_id_type=MESH,
        )

    def relay_p(i, c):
        return pltpu.make_async_remote_copy(
            src_ref=S.at[2 + i, c], dst_ref=S.at[2 + i, c], send_sem=prl.at[c], recv_sem=prc.at[i, c],
            device_id=(e, 2 * (5 - x) + 1), device_id_type=MESH,
        )

    def relay_back(c):
        return pltpu.make_async_remote_copy(
            src_ref=S.at[3, c], dst_ref=S.at[3, c], send_sem=prl.at[c], recv_sem=prc.at[1, c],
            device_id=(e, 2 * NX - 1), device_id_type=MESH,
        )

    @pl.when((core == 1) & (x == 0))
    def _():
        def back(h, _):
            relay_back(2 * h + 1).wait_recv()
            relay_back(2 * h + 1).start()
            return 0

        lax.fori_loop(0, K // 2, back, 0)

    def take(i, c):
        forward_p(i, c).wait_recv()

        @pl.when(core == 1)
        def _():
            @pl.when(((x == 3) & (i == 0)) | ((x == 2) & (i == 1) & (c % 2 == 0)))
            def _():
                relay_p(i, c).start()

            forward_p(i, c).start()

        absorb(2 + i, c, S[2 + i, c])

    def arrivals(t, _):
        late = (x // 3) * (t // (2 * K))
        pairs = (x + 1) // 2 - (1 - x // 2)
        i1, c1 = 0, t
        i2, c2 = 1 - t % 2, t // 2
        i3 = (1 - late) * 2 * (t % 2) + late
        c3 = (1 - late) * (t // 2) + late * (t - 2 * K)
        is1 = (x % 2) * (1 - x // 2)
        is2 = (x // 2) * (1 - x % 2)
        is3 = x // 3
        i = is1 * i1 + is2 * i2 + is3 * i3
        c = is1 * c1 + is2 * c2 + is3 * c3
        take(i, c)
        return 0

    lax.fori_loop(0, K * x, arrivals, 0)

    eye = lax.broadcasted_iota(jnp.int32, (W, W), 0) == lax.broadcasted_iota(jnp.int32, (W, W), 1)

    def write(c):
        return pltpu.make_async_copy(ostage.at[c], out.at[0, 0, :, :, pl.ds(c * W, W)], out_sem.at[c])

    for c in range(K):
        square = acc[1, c * W:(c + 1) * W, c * W:(c + 1) * W].astype(BF16).astype(F32)
        diagonal = jnp.sum(jnp.where(eye, square, 0.0), axis=0, keepdims=True)
        dsend[:, c * W:(c + 1) * W] = -occ[0] * diagonal

    drecv[e] = dsend[...]

    def send_density(k, _):
        pltpu.make_async_remote_copy(
            src_ref=dsend, dst_ref=drecv.at[e], send_sem=ds, recv_sem=dr, device_id=(peer_of(k), s), device_id_type=MESH
        ).start()
        return 0

    lax.fori_loop(1, E, send_density, 0)
    for c in range(K):
        ostage[c, 0] = acc[0, :, c * W:(c + 1) * W].astype(BF16)
        ostage[c, 1] = acc[1, :, c * W:(c + 1) * W].astype(BF16)
        write(c).start()

    wait_bytes(drecv.at[pl.ds(0, E - 1)], dr)
    dens[...] = jnp.sum(drecv[...], axis=0)

    wait_bytes(drecv.at[pl.ds(0, E - 1)], ds)
    for c in range(K):
        write(c).wait()

    for c in range(K):
        wait_bytes(recvs[c].at[pl.ds(0, E - 1)], a1s.at[c])

    def drain(c, _):
        wait_bytes(sigout.at[c, pl.ds(0, E - 1)], a2s.at[c])

        @pl.when(core == 0)
        def _():
            to_core1(c).wait_send()

        @pl.when((core == 1) & (x < NX - 1))
        def _():
            send_p(c, x + 1, 0).wait_send()

            @pl.when(x == 0)
            def _():
                send_p(c, NX - 1, 1).wait_send()

            @pl.when((x == 1) & (c % 2 == 1))
            def _():
                send_p(c, 0, 1).wait_send()

        @pl.when((core == 1) & ((x == 3) | ((x == 2) & (c % 2 == 0))))
        def _():
            relay_p(0, c).wait_send()

        @pl.when((core == 1) & (x == 0) & (c % 2 == 1))
        def _():
            relay_back(c).wait_send()

        @pl.when(core == 1)
        def _():
            def one(i, _):
                forward_p(i, c).wait_send()
                return 0

            lax.fori_loop(0, x, one, 0)

        return 0

    lax.fori_loop(0, K, drain, 0)

    @pl.when(core == 0)
    def _():
        to_partner.wait_send()

    @pl.when(core == 1)
    def _():
        for to_x in range(2, NX):
            @pl.when((x >= 1) & (x < to_x))
            def _(to_x=to_x):
                send_m(to_x).wait_send()
        for i in range(NX - 2):
            @pl.when(x >= i + 2)
            def _(i=i):
                forward_m(i).wait_send()


def solution(mesh):
    E, NS = mesh.shape["energy"], mesh.shape["slab"]
    NY = min(4, E)

    def local(green, inv, coup, phon, off, occ, src, mode, act):
        N = coup.shape[0]
        K = CHUNKS
        R, W, NX = N // E, N // K, NS // 2
        NM, NP = phon.shape[0], src.shape[1]
        sizes = (E, NS, N, K, NM, NP, NY)
        anywhere = pl.BlockSpec(memory_space=pl.ANY)
        smem = pl.BlockSpec(memory_space=pltpu.SMEM)
        vmem = pl.BlockSpec(memory_space=pltpu.VMEM)
        dma = pltpu.SemaphoreType.DMA
        matrix = pltpu.VMEM((2, N, N), BF16)
        scratch = [
            *[pltpu.VMEM((E, 2, R, W), BF16) for _ in range(K)],
            pltpu.VMEM((K, E, R, 2 * W), BF16),
            pltpu.VMEM((1 + NX, K, N, 2 * W), BF16),
            pltpu.VMEM((K, N, 2 * W), BF16),
            pltpu.VMEM((1 + NX, 2, N, N), BF16),
            pltpu.VMEM((1 + NX, K, 2 * W, N), BF16),
            pltpu.VMEM((1 + NX, K, 2 * W, N), BF16),
            matrix,
            pltpu.VMEM((N, N), BF16),
            pltpu.VMEM((K, NM, R, W), F32),
            matrix,
            matrix,
            matrix,
            pltpu.VMEM((NX - 2, 2, N, N), BF16),
            matrix,
            pltpu.VMEM((2, N, N), F32),
            pltpu.VMEM((K, 2, N, W), BF16),
            pltpu.VMEM((1, N), F32),
            pltpu.VMEM((E, 1, N), F32),
            dma((2,)), dma((K,)),
            dma((K,)), dma((K,)), dma((K,)), dma((K,)),
            dma, dma,
            dma((NX,)), dma((NX - 2,)), dma((NX - 2,)),
            dma((K,)), dma((K,)),
            dma((2, K)), dma((NX - 1, K)), dma((K,)), dma((NX - 1, K)),
            dma((K,)), dma, dma,
        ]
        return pl.pallas_call(
            functools.partial(kernel, sizes),
            out_shape=(
                jax.ShapeDtypeStruct((1, 1, 2, N, N), BF16),
                jax.ShapeDtypeStruct((1, N), F32),
            ),
            in_specs=[anywhere, anywhere, anywhere, vmem, smem, smem, smem, smem],
            out_specs=(anywhere, vmem),
            scratch_shapes=scratch,
            compiler_params=pltpu.CompilerParams(
                collective_id=0, has_side_effects=True, vmem_limit_bytes=60 * 1024 * 1024
            ),
            name="born",
        )(green, inv, coup, phon, off, occ, src * NM + mode, act)

    in_specs = (
        P("energy", "slab", None, None, None),
        P("slab", None, None, None),
        P(),
        P(None, "energy", None),
        P("energy"),
        P("energy"),
        P(),
        P(),
        P("energy"),
    )
    out_specs = (P("energy", "slab", None, None, None), P("slab", None))
    return jax.shard_map(local, mesh=mesh, in_specs=in_specs, out_specs=out_specs, check_vma=False)
```
